32 devices in a mesh: groups: 2 (over x), seq: 16 (over z, y, core).
Axes of the slice: x: 2, y: 2, z: 4, core: 2. Of those that a mesh axis runs over, the one named last changes fastest.
Arguments:
- hidden_in: bfloat16 [32768, 2048], P(('groups', 'seq')), parts along dimension 0, may hold values from -6 to 6
- queries: bfloat16 [32768, 1024], P(('groups', 'seq')), parts along dimension 0, may hold values from -6 to 6
- kv_weight: bfloat16 [2048, 2048], replicated, may hold values from -0.125 to 0.125
- level_weight: float32 [16, 8], replicated, may hold values from 0.3 to 3
Outputs:
- attended: bfloat16 [32768, 1024], P(('groups', 'seq')), parts along dimension 0
The draws below stay inside these ranges and needn't reach their ends.
There are 2 independent parts, one for each index of `groups`. The reference program is written for one: setup_inputs(seed, part) draws one part's arguments, and reference() takes and returns one part's arrays. A program takes and returns all parts, laid end to end along the dimension named above; an argument that names none is the same for every part. Nothing has to cross between parts.
All inputs are finite; a program needn't handle non-finite values.
Results may differ from the reference program's by a relative error of at most 0.0034.
Values sent between devices are 32-bit elements; how exact they have to be, the bound alone decides.
No kernel may reach another device: no remote copies, remote signals or barrier semaphores. Data moves between devices by JAX's collectives and lax.ppermute only.
A program may use at most 128 MiB of HBM per device.

```python
import math
import jax
import jax.numpy as jnp
from jax import lax

D = 2048
HEADS = 8
HEAD = 128
SPAN = 64
LEVELS = 16
TOKENS = 16384


def steps_of(rng, shape, shards, least, high):
    factor_of = 1.0
    for axis_at, blocks in shards:
        steps = jax.random.uniform(jax.random.fold_in(jax.random.fold_in(rng, 6), axis_at), (blocks,), jnp.float32, least / len(shards), high / len(shards))
        factor_of = factor_of * jnp.repeat(jnp.exp(steps), shape[axis_at] // blocks).reshape((-1,) + (1,) * (len(shape) - 1 - axis_at))
    return factor_of


def noise(stream_key, shape, spread, most, cuts=(), kind=jnp.bfloat16):
    values = spread * jax.random.normal(stream_key, shape, jnp.float32)
    if cuts:
        values = values * steps_of(stream_key, shape, cuts, -0.22, 0.18)
    return jnp.clip(values, -most, most).astype(kind)


def setup_inputs(seed: int = 0, part: int = 0) -> dict:
    streams_of = jax.random.split(jax.random.key(seed), 5)
    part_keys = jax.random.split(jax.random.fold_in(streams_of[4], part), 5)
    hidden_in = noise(part_keys[0], (TOKENS, D), 1.0, 6.0, ((0, 16),))
    queries = noise(part_keys[1], (TOKENS, HEADS * HEAD), 1.0, 6.0, ((0, 16),))
    kv_weight = noise(streams_of[2], (D, 2 * HEADS * HEAD), D ** -0.5, 0.125)
    level_weight = jnp.clip(jnp.exp(jax.random.uniform(streams_of[3], (LEVELS, HEADS), jnp.float32, math.log(0.3), math.log(3.0))), 0.3, 3.0)
    return dict(hidden_in=hidden_in, queries=queries, kv_weight=kv_weight, level_weight=level_weight)


def reference(hidden_in, queries, kv_weight, level_weight):
    tokens = hidden_in.shape[0]
    spans = tokens // SPAN
    width = HEADS * HEAD
    nbits = LEVELS - 1
    highest = lax.Precision.HIGHEST
    kv = jnp.dot(hidden_in, kv_weight, preferred_element_type=jnp.float32).astype(jnp.bfloat16)
    keys = kv[:, :width].reshape(spans, SPAN, HEADS, HEAD)
    values = kv[:, width:].reshape(spans, SPAN, HEADS, HEAD)
    query_blocks = queries.reshape(spans, SPAN, HEADS, HEAD)
    levels = jnp.arange(nbits, dtype=jnp.int32)
    lengths = 2.0 ** levels.astype(jnp.float32) * SPAN
    scales = level_weight[1:] / jnp.sqrt(lengths)[:, None]
    causal = jnp.tril(jnp.ones((SPAN, SPAN), jnp.float32))
    diag_scale = level_weight[0] / jnp.sqrt(jnp.float32(SPAN * HEAD))

    def advance(carry, inputs):
        running, done = carry
        key_c, val_c, query_c, index = inputs
        bits = (jnp.right_shift(index, levels) & 1).astype(jnp.float32)
        coef = bits[:, None] * scales
        state = jnp.einsum('lh,lhab->hab', coef, done, precision=highest)
        query_f = query_c.astype(jnp.float32)
        key_f = key_c.astype(jnp.float32)
        val_f = val_c.astype(jnp.float32)
        inter = jnp.einsum('tha,hab->thb', query_f, state, precision=highest) / jnp.sqrt(jnp.float32(HEAD))
        scores = jnp.einsum('tha,sha->hts', query_f, key_f, precision=highest)
        scores = (scores * diag_scale[:, None, None] * causal[None]).astype(jnp.bfloat16)
        intra = jnp.einsum('hts,shb->thb', scores.astype(jnp.float32), val_f, precision=highest)
        result = (intra + inter).astype(jnp.bfloat16)
        span_state = jnp.einsum('tha,thb->hab', key_f, val_f, precision=highest)
        running = running + span_state[None]
        powers = jnp.left_shift(jnp.int32(1), levels)
        complete = (index + 1) % powers == 0
        done = jnp.where(complete[:, None, None, None], running, done)
        running = jnp.where(complete[:, None, None, None], jnp.zeros_like(running), running)
        return ((running, done), result)
    start = jnp.zeros((nbits, HEADS, HEAD, HEAD), jnp.float32)
    order = jnp.arange(spans, dtype=jnp.int32)
    _, results = lax.scan(advance, (start, start), (keys, values, query_blocks, order))
    return results.reshape(tokens, width)
```

```python
import functools
import math

import jax
import jax.numpy as jnp
from jax import lax
from jax.experimental import pallas as pl
from jax.experimental.pallas import tpu as pltpu
from jax.sharding import PartitionSpec as P


HEAD = 128
SPAN = 64
CHUNK = 256
PAIR = 2 * HEAD
MIB = 1 << 20

BF16 = jnp.bfloat16
F32 = jnp.float32
VMEM = pl.BlockSpec(memory_space=pltpu.VMEM)
HBM = pl.BlockSpec(memory_space=pltpu.MemorySpace.HBM)
SMEM = pl.BlockSpec(memory_space=pltpu.SMEM)


def in_hbm(x):
    return pltpu.with_memory_space_constraint(x, pltpu.MemorySpace.HBM)


def own_pair():
    index = lax.axis_index("seq")
    return (index & 1) * 2 + (index >> 1 & 1)


def dot(a, b):
    return jnp.dot(a, b, preferred_element_type=F32)


def outer(a, b):
    return lax.dot_general(a, b, (((0,), (0,)), ((), ())), preferred_element_type=F32)


def pair_states(k_ref, v_ref, column, s_ref, first):
    for i in range(2):
        at = slice(column + i * HEAD, column + (i + 1) * HEAD)
        s_ref[first + i] = outer(k_ref[:, at], v_ref[:, at])


def first_kernel(h_hbm, w_hbm, k_ref, v_ref, s_ref, h_ref, w_rest, w_first, h_sem, w_sem):
    tokens, width = h_hbm.shape[0], w_hbm.shape[1] // 2
    rows = tokens // 4
    own = own_pair()

    def load_w(n):
        pair, part = n // 2, n % 2
        column = pl.multiple_of((own ^ (3 - pair)) * PAIR + part * width, PAIR)
        target = w_first.at[n] if n < 4 else w_rest.at[n - 4]
        return pltpu.make_async_copy(w_hbm.at[:, pl.ds(column, PAIR)], target, w_sem.at[n])

    def load_h(r):
        at = pl.ds(r * rows, rows)
        return pltpu.make_async_copy(h_hbm.at[at, :], h_ref.at[at, :], h_sem.at[r])

    weights = [load_w(n) for n in range(8)]
    hidden = [load_h(r) for r in range(4)]
    for copy in [weights[0], hidden[0], weights[1]] + hidden[1:] + weights[2:]:
        copy.start()
    weights[0].wait()
    for r in range(4):
        at = slice(r * rows, (r + 1) * rows)
        hidden[r].wait()
        k_ref[at, :PAIR] = dot(h_ref[at, :], w_first[0]).astype(BF16)
        if r == 0:
            weights[1].wait()
        v_ref[at, :PAIR] = dot(h_ref[at, :], w_first[1]).astype(BF16)
    weights[2].wait()
    k_ref[:, PAIR:] = dot(h_ref[...], w_first[2]).astype(BF16)
    weights[3].wait()
    v_ref[:, PAIR:] = dot(h_ref[...], w_first[3]).astype(BF16)
    pair_states(k_ref, v_ref, 0, s_ref, 0)
    pair_states(k_ref, v_ref, PAIR, s_ref, 2)
    for n in range(4, 8):
        weights[n].wait()


def next_kernel(pair, h_ref, w_rest, k_ref, v_ref, s_ref):
    k_ref[...] = dot(h_ref[...], w_rest[2 * pair]).astype(BF16)
    v_ref[...] = dot(h_ref[...], w_rest[2 * pair + 1]).astype(BF16)
    pair_states(k_ref, v_ref, 0, s_ref, 0)


def project(hidden_in, kv_weight):
    tokens, depth = hidden_in.shape
    bf = lambda *shape: jax.ShapeDtypeStruct(shape, BF16)
    state = lambda n: jax.ShapeDtypeStruct((n, HEAD, HEAD), F32)
    flops = 2 * tokens * depth * PAIR
    k0, v0, s0, hidden, w_rest = pl.pallas_call(
        first_kernel,
        in_specs=[HBM, HBM],
        out_specs=[VMEM] * 5,
        out_shape=[bf(tokens, 2 * PAIR), bf(tokens, 2 * PAIR), state(4), bf(tokens, depth), bf(4, depth, PAIR)],
        scratch_shapes=[
            pltpu.VMEM((4, depth, PAIR), BF16),
            pltpu.SemaphoreType.DMA((4,)),
            pltpu.SemaphoreType.DMA((8,)),
        ],
        cost_estimate=pl.CostEstimate(flops=4 * flops, bytes_accessed=12 * MIB, transcendentals=0),
        compiler_params=pltpu.CompilerParams(vmem_limit_bytes=20 * MIB),
        name="kv_first",
    )(in_hbm(hidden_in), in_hbm(kv_weight))
    parts = [(k0, v0, s0)]
    for pair in range(2):
        parts.append(
            pl.pallas_call(
                functools.partial(next_kernel, pair),
                in_specs=[VMEM, VMEM],
                out_specs=[VMEM] * 3,
                out_shape=[bf(tokens, PAIR), bf(tokens, PAIR), state(2)],
                cost_estimate=pl.CostEstimate(flops=2 * flops, bytes_accessed=8 * MIB, transcendentals=0),
                compiler_params=pltpu.CompilerParams(vmem_limit_bytes=4 * MIB),
                name="kv_next",
            )(hidden, w_rest)
        )
    return parts


def split_state(state):
    high = state.astype(BF16)
    low = (state - high.astype(F32)).astype(BF16)
    return jnp.concatenate([high, low], axis=0)


def local_kernel(first, own_ref, lw_ref, q_ref, k_ref, v_ref, o_ref, mask_ref):
    head = pl.program_id(0)
    tokens = q_ref.shape[0]
    chunks = tokens // CHUNK
    actual = (own_ref[0] ^ (3 - (first + head) // 2)) * 2 + head % 2
    scale = lambda level: lw_ref[actual, 1 + level] * F32(1.0 / math.sqrt(2**level * SPAN * HEAD))
    diagonal = lw_ref[actual, 0] * F32(1.0 / math.sqrt(SPAN * HEAD))
    row = lax.broadcasted_iota(jnp.int32, (CHUNK, CHUNK), 0)
    col = lax.broadcasted_iota(jnp.int32, (CHUNK, CHUNK), 1)
    apart = (row // SPAN) ^ (col // SPAN)
    mask = jnp.where(apart == 0, diagonal, jnp.where(apart == 1, scale(0), scale(1)))
    mask_ref[...] = jnp.where(row >= col, mask, 0.0)
    lanes = pl.ds(pl.multiple_of(head * HEAD, HEAD), HEAD)
    rows = [pl.ds(c * CHUNK, CHUNK) for c in range(chunks)]
    sums = {}
    for c in range(chunks - 1):
        sums[(0, c)] = outer(k_ref[rows[c], lanes], v_ref[rows[c], lanes])
    levels = chunks.bit_length() - 1
    for level in range(levels - 1):
        for b in range((chunks >> (level + 1)) - 1):
            sums[(level + 1, b)] = sums[(level, 2 * b)] + sums[(level, 2 * b + 1)]
    for c in range(chunks):
        q = q_ref[rows[c], :]
        k = k_ref[rows[c], lanes]
        v = v_ref[rows[c], lanes]
        scores = lax.dot_general(q, k, (((1,), (1,)), ((), ())), preferred_element_type=F32)
        scores = (scores * mask_ref[...]).astype(BF16)
        result = dot(scores, v)
        if c:
            state = None
            for level in range(levels):
                if (c >> level) & 1:
                    term = scale(level + 2) * sums[(level, (c >> level) - 1)]
                    state = term if state is None else state + term
            result = result + dot(jnp.concatenate([q, q], axis=1), split_state(state))
        o_ref[rows[c], :] = result


def local_part(own, level_weight, queries, keys, values, first):
    tokens = queries.shape[0]
    heads = keys.shape[1] // HEAD
    spec = pltpu.PrefetchScalarGridSpec(
        num_scalar_prefetch=1,
        grid=(heads,),
        in_specs=[
            SMEM,
            pl.BlockSpec((tokens, HEAD), lambda j, own: (0, (own[0] ^ (3 - (first + j) // 2)) * 2 + j % 2)),
            VMEM,
            VMEM,
        ],
        out_specs=pl.BlockSpec((tokens, HEAD), lambda j, own: (0, j)),
        scratch_shapes=[pltpu.VMEM((CHUNK, CHUNK), F32)],
    )
    return pl.pallas_call(
        functools.partial(local_kernel, first),
        grid_spec=spec,
        out_shape=jax.ShapeDtypeStruct((tokens, heads * HEAD), F32),
        cost_estimate=pl.CostEstimate(flops=heads * 200 * 10**6, bytes_accessed=heads * MIB, transcendentals=0),
        compiler_params=pltpu.CompilerParams(vmem_limit_bytes=12 * MIB),
        name="local_part",
    )(own, level_weight, queries, keys, values)


def factors(lw_ref, level, tokens, pair):
    own = own_pair()
    head = (own ^ (3 - pair)) * 2
    at = 1 + (tokens // SPAN).bit_length() - 1 + level
    scale = F32(1.0 / math.sqrt(2**level * tokens * HEAD))
    return [lw_ref[head + i, at] * scale for i in range(2)]


def taken(level):
    return (lax.axis_index("seq") >> level & 1).astype(F32)


def add_kernel(a_ref, b_ref, o_ref):
    o_ref[...] = a_ref[...] + b_ref[...]


def widen_kernel(tokens, lw_ref, s_ref, half_ref, quarter_ref, *refs):
    gots, (send_ref, far_ref) = refs[:-2], refs[-2:]
    near = factors(lw_ref, 1, tokens, 3)
    levels = [factors(lw_ref, 2 + n, tokens, 3) for n in range(len(gots))]
    for i in range(2):
        far = sum((taken(2 + n) * levels[n][i]) * gots[n][i] for n in range(len(gots)))
        send_ref[i] = far + ((1.0 - taken(1)) * near[i]) * (s_ref[i] + half_ref[2 + i])
        far_ref[i] = far + (taken(1) * near[i]) * quarter_ref[i]


def share_kernel(tokens, lw_ref, s2_ref, s3_ref, far2_ref, far3_ref, send_ref):
    for pair, far_ref, s_ref in ((2, far2_ref, s2_ref), (3, far3_ref, s3_ref)):
        near = factors(lw_ref, 0, tokens, pair)
        for i in range(2):
            send_ref[2 * pair - 4 + i] = far_ref[i] + ((1.0 - taken(0)) * near[i]) * s_ref[i]


def small(kernel, heads, count, specs, *operands):
    return pl.pallas_call(
        kernel,
        in_specs=specs,
        out_specs=[VMEM] * count,
        out_shape=[jax.ShapeDtypeStruct((heads, HEAD, HEAD), F32)] * count,
        cost_estimate=pl.CostEstimate(flops=10**6, bytes_accessed=MIB // 2, transcendentals=0),
        compiler_params=pltpu.CompilerParams(vmem_limit_bytes=2 * MIB),
    )(*operands)


def final_kernel(first, own_ref, lw_ref, q_ref, a_ref, r_ref, *rest):
    o_ref = rest[-1]
    head = pl.program_id(0)
    tokens = q_ref.shape[0]
    q = q_ref[...]
    state = r_ref[0]
    if first >= 4:
        near = factors(lw_ref, 0, tokens, first // 2)
        weight = taken(0) * jnp.where(head == 0, near[0], near[1])
        state = state + weight * rest[0][0]
    far = dot(jnp.concatenate([q, q], axis=1), split_state(state))
    o_ref[...] = (a_ref[...] + far).astype(BF16)


def final_part(own, level_weight, queries, local, remote, first, half=None, previous=None):
    tokens, width = queries.shape
    heads = local.shape[1] // HEAD
    place = lambda j, own: (0, (own[0] ^ (3 - (first + j) // 2)) * 2 + j % 2)
    in_specs = [
        SMEM,
        pl.BlockSpec((tokens, HEAD), place),
        pl.BlockSpec((tokens, HEAD), lambda j, own: (0, j)),
        pl.BlockSpec((1, HEAD, HEAD), lambda j, own: (j, 0, 0)),
    ]
    operands = [level_weight, queries, local, remote]
    if half is not None:
        in_specs.append(pl.BlockSpec((1, HEAD, HEAD), lambda j, own: (first - 4 + j, 0, 0)))
        operands.append(half)
    aliases = {}
    if previous is not None:
        in_specs.append(HBM)
        operands.append(previous)
        aliases = {len(operands): 0}
    return pl.pallas_call(
        functools.partial(final_kernel, first),
        grid_spec=pltpu.PrefetchScalarGridSpec(
            num_scalar_prefetch=1,
            grid=(heads,),
            in_specs=in_specs,
            out_specs=pl.BlockSpec((tokens, HEAD), place),
        ),
        out_shape=jax.ShapeDtypeStruct((tokens, width), BF16),
        input_output_aliases=aliases,
        cost_estimate=pl.CostEstimate(flops=heads * 70 * 10**6, bytes_accessed=heads * MIB, transcendentals=0),
        compiler_params=pltpu.CompilerParams(vmem_limit_bytes=12 * MIB),
        name="final_part",
    )(own, *operands)


def exchange(x, level):
    size = lax.axis_size("seq")
    return lax.ppermute(x, "seq", [(i, i ^ 1 << level) for i in range(size)])


def upward(x, level):
    size = lax.axis_size("seq")
    return lax.ppermute(x, "seq", [(i, i + (1 << level)) for i in range(size) if not i >> level & 1])


def layer(hidden_in, queries, kv_weight, level_weight):
    tokens = hidden_in.shape[0]
    depth = lax.axis_size("seq").bit_length() - 1
    own = own_pair().reshape(1)
    weights = level_weight.T

    (k0, v0, s0), (k2, v2, s2), (k3, v3, s3) = project(hidden_in, kv_weight)
    half = exchange(s0, 0)
    quarter = exchange(s2 + half[:2], 1)
    block = s3 + half[2:] + quarter

    local0 = local_part(own, weights, queries, k0, v0, 0)
    local2 = local_part(own, weights, queries, k2, v2, 4)
    local3 = local_part(own, weights, queries, k3, v3, 6)

    gots = []
    for level in range(2, depth - 1):
        gots.append(exchange(block, level))
        (block,) = small(add_kernel, 2, 1, [VMEM] * 2, block, gots[-1])
    gots.append(upward(block, depth - 1))
    send, far3 = small(
        functools.partial(widen_kernel, tokens), 2, 2,
        [SMEM] + [VMEM] * (3 + len(gots)), weights, s3, half, quarter, *gots,
    )
    far2 = exchange(send, 1)
    (send,) = small(
        functools.partial(share_kernel, tokens), 4, 1,
        [SMEM] + [VMEM] * 4, weights, s2, s3, far2, far3,
    )
    far01 = exchange(send, 0)

    out = final_part(own, weights, queries, local3, far3, 6, half)
    out = final_part(own, weights, queries, local2, far2, 4, half, out)
    return final_part(own, weights, queries, local0, far01, 0, None, out)


def solution(mesh):
    in_specs = (P(("groups", "seq"), None), P(("groups", "seq"), None), P(), P())
    out_specs = P(("groups", "seq"), None)
    return jax.shard_map(layer, mesh=mesh, in_specs=in_specs, out_specs=out_specs, check_vma=False)
```
